512 devices in a mesh: wide: 64 (over z, y), grp: 8 (over x, core).
Axes of the slice: x: 4, y: 4, z: 16, core: 2. Of those that a mesh axis runs over, the one named last changes fastest.
Arguments:
- amplitudes: bfloat16 [512, 131072], P(('wide', 'grp')), may hold values from -6 to 6
- amplitude_live: int32 [512, 1024], replicated, may hold values from 0 to 1, as said below
- integrals: bfloat16 [2048, 131072], P('grp', 'wide'), may hold values from -0.0234375 to 0.0234375
- integral_live: int32 [16, 1024], P('grp', 'wide'), may hold values 0 or 1
Outputs:
- ladder: bfloat16 [512, 2048], P(('wide', 'grp'))
The draws below stay inside these ranges and needn't reach their ends.
Inputs may be any that keep to these rules, and one draw needn't show every extreme that they name: `amplitude_live`: entries are 0 or 1. In every row b, among the 16 cd tiles c with c // 16 equal to one index of wide, at most 12 are 1; in every row exactly 12 for at least one such index.
All inputs are finite; a program needn't handle non-finite values. No bound on the sum of `integral_live` on one device may be relied on, other than what follows from the above.
Results may differ from the reference program's by a relative error of at most 0.0018.
Values may be sent and summed in bfloat16 or wider, within the bound.
No kernel may reach another device: no remote copies, remote signals or barrier semaphores. Data moves between devices by JAX's collectives and lax.ppermute only.
A program may use at most 64 MiB of HBM per device.

```python
import jax
import jax.numpy as jnp
from jax import lax

TW = 128
ROWS_DEV = 1
CD_DEV = 16
CAP = 12
NBLK = 512
IJ = 512
NCD = 1024
NAB = 16
N_WIDE = 64


def draw_amplitude_live(key, part):
    key_score = jax.random.fold_in(key, 11)
    key_count = jax.random.fold_in(key, 12)
    key_full = jax.random.fold_in(key, 13)
    scores = jax.random.randint(key_score, (NBLK, N_WIDE, CD_DEV), 0, 65536) * CD_DEV + jnp.arange(CD_DEV, dtype=jnp.int32)
    ranking = jnp.argsort(jnp.argsort(scores, axis=-1), axis=-1)
    counts = jax.random.randint(key_count, (NBLK, N_WIDE), 1, CAP + 1)
    fullest = jax.random.randint(key_full, (NBLK, 1), 0, N_WIDE)
    counts = jnp.where(jnp.arange(N_WIDE, dtype=jnp.int32)[None, :] == fullest, CAP, counts)
    live = (ranking < counts[:, :, None]).astype(jnp.int32)
    return live.reshape(NBLK, N_WIDE * CD_DEV)


def with_ends(values, key, smallest, top_value):
    index_at = [jax.random.randint(jax.random.fold_in(key, axis), (), 0, length) for axis, length in enumerate(values.shape)]
    main_axis = values.shape.index(max(values.shape))
    beside = index_at[:main_axis] + [(index_at[main_axis] + 1) % values.shape[main_axis]] + index_at[main_axis + 1:]
    return values.at[tuple(index_at)].set(smallest).at[tuple(beside)].set(top_value)


def steps_of(stream_key, dims, split, low, top_value):
    gain, own = 1.0, jax.random.fold_in(stream_key, 6)
    for position, parts in split:
        steps = jnp.exp(jax.random.uniform(jax.random.fold_in(own, position), (parts,), jnp.float32, low / len(split), top_value / len(split)))
        gain = gain * jnp.repeat(steps, dims[position] // parts).reshape([-1 if axis == position else 1 for axis in range(len(dims))])
    return gain


def normal_values(key, dims, scale, most, pieces=(), held_as=jnp.bfloat16):
    drawn = jax.random.normal(key, dims, jnp.float32) * scale
    if len(pieces) > 0:
        drawn = steps_of(key, dims, pieces, -0.22, 0.18) * drawn
    return jnp.clip(drawn, min=-most, max=most).astype(held_as)


def setup_inputs(seed: int = 0) -> dict:
    key_of = jax.random.split(jax.random.key(seed), 5)
    amplitudes = normal_values(key_of[0], (IJ, NCD * TW), 1.0, 6.0, ((0, 512),))
    amplitude_live = draw_amplitude_live(jax.random.fold_in(key_of[4], 71), 0)
    integrals = normal_values(key_of[2], (NAB * TW, NCD * TW), (NCD * TW // 2) ** -0.5, 0.0234375, ((0, 8), (1, 64)))
    integral_live = with_ends((jax.random.randint(key_of[3], (NAB, NCD), 0, 4) < 3).astype(jnp.int32), jax.random.fold_in(key_of[3], 1), 0, 1)
    return {"amplitudes": amplitudes, "amplitude_live": amplitude_live, "integrals": integrals, "integral_live": integral_live}


def reference(amplitudes, amplitude_live, integrals, integral_live):
    amp_mask = amplitude_live.astype(amplitudes.dtype)
    amp_used = (amplitudes.reshape(NBLK, ROWS_DEV, NCD, TW) * amp_mask[:, None, :, None]).reshape(IJ, NCD * TW)
    int_mask = integral_live.astype(integrals.dtype)
    int_used = (integrals.reshape(NAB, TW, NCD, TW) * int_mask[:, None, :, None]).reshape(NAB * TW, NCD * TW)
    ladder = lax.dot_general(amp_used, int_used, (((1,), (1,)), ((), ())), preferred_element_type=jnp.float32)
    return ladder.astype(jnp.bfloat16)
```

```python
import functools

import jax
import jax.numpy as jnp
from jax import lax
from jax.experimental import pallas as pl
from jax.experimental.pallas import tpu as pltpu
from jax.sharding import Mesh, PartitionSpec as P

TW = 128
NZ, NY, NX, NC = 16, 4, 4, 2
NW = NZ * NY
CT = 16
CAP = 12
DROP = CT - CAP
F32 = jnp.float32
BF16 = jnp.bfloat16


def iota(shape, dim):
    return lax.broadcasted_iota(jnp.int32, shape, dim)


def dot(a, b):
    return lax.dot_general(a, b, (((1,), (0,)), ((), ())), preferred_element_type=F32)


def before_matrix():
    rows, cols = iota((TW, TW), 0), iota((TW, TW), 1)
    same = (rows // CT) == (cols // CT)
    return jnp.where(same & (rows < cols), 1.0, 0.0).astype(BF16)


def pack_kernel(me_ref, live_ref, amp_ref, out_ref):
    sub = me_ref[0] % 8
    live = live_ref[...].astype(F32)
    row = jnp.sum(jnp.where(iota(live.shape, 0) == sub, live, 0.0), axis=0, keepdims=True)
    dead = jnp.broadcast_to(1.0 - row, (8, NW * CT)).astype(BF16)
    before = before_matrix()
    lanes = 2 * TW
    out_row, col = iota((lanes, lanes), 0), iota((lanes, lanes), 1)
    slot = jnp.where(out_row // CT == col // CT, out_row % CT, -7).astype(F32)
    tile = (iota((1, lanes), 1) % CT).astype(F32)
    for q in range(4):
        dead_q = dead[:, q * lanes : (q + 1) * lanes]
        count = jnp.concatenate([dot(dead_q[:, :TW], before), dot(dead_q[:, TW:], before)], axis=1)[0:1]
        is_dead = dead_q[0:1].astype(F32)
        dropped = (is_dead > 0.5) & (count < DROP - 0.5)
        key = jnp.where(dropped, -1.0, tile - jnp.minimum(count, float(DROP)))
        pick = jnp.where(slot == key, 1.0, 0.0).astype(BF16)
        packed = dot(pick, amp_ref[q * lanes : (q + 1) * lanes, :]).astype(BF16)
        for i in range(16):
            z, y = q * 4 + i // NY, i % NY
            out_ref[y * NZ + z] = packed[i * CT : i * CT + CAP, :]


def pack(me, live, amp_tiles):
    return pl.pallas_call(
        pack_kernel,
        out_shape=jax.ShapeDtypeStruct((NW, CAP, TW), BF16),
        grid_spec=pltpu.PrefetchScalarGridSpec(
            num_scalar_prefetch=1,
            grid=(1,),
            in_specs=[
                pl.BlockSpec((8, NW * CT), lambda i, me: (me[0] // 8, 0)),
                pl.BlockSpec((NW * CT, TW), lambda i, me: (0, 0)),
            ],
            out_specs=pl.BlockSpec((NW, CAP, TW), lambda i, me: (0, 0, 0)),
        ),
        name="pack",
    )(me, live, amp_tiles)


def ladder_kernel(ids_ref, live_ref, amp_ref, own_ref, other_ref, out_ref, used_ref):
    wide, core = ids_ref[0], ids_ref[1]
    rows = NX * NW
    r, g = iota((rows, 512), 0), iota((rows, 512), 1)
    rx, ry, rz = r // NW, (r // NZ) % NY, r % NZ
    source = ((rz * NY + ry) * NX + rx) * NC + core
    pick = jnp.where(g == source, 1.0, 0.0).astype(BF16)
    live = dot(pick, live_ref[...].astype(F32).astype(BF16)).astype(BF16)
    base = (wide % 8) * CT
    lane, c = iota((TW, TW), 0), iota((TW, TW), 1)
    take = jnp.where((lane == base + c) & (c < CT), 1.0, 0.0).astype(BF16)
    prior = jnp.where((lane >= base) & (lane < base + c) & (c < CT), 1.0, 0.0).astype(BF16)
    here = dot(live, take)
    count = dot((1.0 - live.astype(F32)).astype(BF16), prior)
    code = jnp.where(here > 0.5, jnp.minimum(count, float(DROP)), 9.0).astype(BF16)
    spread_row, spread_col = iota((TW, CT * TW), 0), iota((TW, CT * TW), 1)
    spread = jnp.where(spread_row == spread_col // TW, 1.0, 0.0).astype(BF16)
    codes = dot(code, spread).astype(BF16)
    for t in range(CT):
        code_t = codes[:, t * TW : (t + 1) * TW]
        value = jnp.zeros((rows, TW), BF16)
        for d in range(DROP + 1):
            if 0 <= t - d < CAP:
                value = jnp.where(code_t == d, amp_ref[t - d], value)
        used_ref[:, t * TW : (t + 1) * TW] = value
    used = used_ref[...]
    for ref, column in ((own_ref, core), (other_ref, 1 - core)):
        sums = lax.dot_general(used, ref[...], (((1,), (1,)), ((), ())), preferred_element_type=F32)
        for y in range(NY):
            for x in range(NX):
                at = x * NW + y * NZ
                out_ref[y, column, x * NZ : (x + 1) * NZ, :] = sums[at : at + NZ, :]


def ladder(ids, live, amp, own, other):
    whole = lambda *dims: pl.BlockSpec(dims, lambda i, ids: (0,) * len(dims))
    return pl.pallas_call(
        ladder_kernel,
        out_shape=jax.ShapeDtypeStruct((NY, NC, NX * NZ, 256), F32),
        grid_spec=pltpu.PrefetchScalarGridSpec(
            num_scalar_prefetch=1,
            grid=(1,),
            in_specs=[
                pl.BlockSpec((512, TW), lambda i, ids: (0, ids[0] // 8)),
                whole(CAP, NX * NW, TW),
                whole(256, CT * TW),
                whole(256, CT * TW),
            ],
            out_specs=whole(NY, NC, NX * NZ, 256),
            scratch_shapes=[pltpu.VMEM((NX * NW, CT * TW), BF16)],
        ),
        compiler_params=pltpu.CompilerParams(vmem_limit_bytes=40 * 1024 * 1024),
        name="ladder",
    )(ids, live, amp, own, other)


def per_device(amplitudes, amplitude_live, integrals, integral_live):
    wide = lax.axis_index("z") * NY + lax.axis_index("y")
    core = lax.axis_index("c")
    me = (wide * NX + lax.axis_index("x")) * NC + core
    mask = integral_live.astype(BF16)
    own = (integrals.reshape(2, TW, CT, TW) * mask[:, None, :, None]).reshape(2 * TW, CT * TW)
    other = lax.ppermute(own, "c", [(0, 1), (1, 0)])
    packed = pack(me.reshape(1), amplitude_live, amplitudes.reshape(NW * CT, TW))
    arrived = lax.all_to_all(packed, ("y", "z"), 0, 0, tiled=True)
    gathered = lax.all_gather(arrived.transpose(1, 0, 2), "x", axis=1, tiled=True)
    sums = ladder(jnp.stack([wide, core]), amplitude_live, gathered, own, other)
    sums = lax.all_to_all(sums, "y", 0, 0, tiled=True).sum(axis=0)
    sums = lax.all_to_all(sums.transpose(1, 0, 2), ("x", "z"), 0, 0, tiled=True)
    return sums.reshape(NX, NZ, NC * 256).sum(axis=1).reshape(1, NX * NC * 256).astype(BF16)


def solution(mesh):
    fine = Mesh(mesh.devices.reshape(NZ, NY, NX, NC), ("z", "y", "x", "c"))
    wide, grp = ("z", "y"), ("x", "c")
    return jax.shard_map(
        per_device,
        mesh=fine,
        in_specs=(P(wide + grp, None), P(), P(grp, wide), P(grp, wide)),
        out_specs=P(wide + grp, None),
        check_vma=False,
    )
```

```python
import functools

import jax
import jax.numpy as jnp
from jax import lax
from jax.experimental import pallas as pl
from jax.experimental.pallas import tpu as pltpu
from jax.sharding import Mesh, PartitionSpec as P

TW = 128
NZ, NY, NX, NC = 16, 4, 4, 2
NW = NZ * NY
CT = 16
CAP = 12
DROP = CT - CAP
F32 = jnp.float32
BF16 = jnp.bfloat16


def iota(shape, dim):
    return lax.broadcasted_iota(jnp.int32, shape, dim)


def dot(a, b):
    return lax.dot_general(a, b, (((1,), (0,)), ((), ())), preferred_element_type=F32)


def before_matrix():
    rows, cols = iota((TW, TW), 0), iota((TW, TW), 1)
    same = (rows // CT) == (cols // CT)
    return jnp.where(same & (rows < cols), 1.0, 0.0).astype(BF16)


def pack_kernel(me_ref, live_ref, amp_ref, out_ref):
    sub = me_ref[0] % 8
    live = live_ref[...].astype(F32)
    row = jnp.sum(jnp.where(iota(live.shape, 0) == sub, live, 0.0), axis=0, keepdims=True)
    dead = jnp.broadcast_to(1.0 - row, (8, NW * CT)).astype(BF16)
    before = before_matrix()
    lanes = 2 * TW
    out_row, col = iota((lanes, lanes), 0), iota((lanes, lanes), 1)
    slot = jnp.where(out_row // CT == col // CT, out_row % CT, -7).astype(F32)
    tile = (iota((1, lanes), 1) % CT).astype(F32)
    for q in range(4):
        dead_q = dead[:, q * lanes : (q + 1) * lanes]
        count = jnp.concatenate([dot(dead_q[:, :TW], before), dot(dead_q[:, TW:], before)], axis=1)[0:1]
        is_dead = dead_q[0:1].astype(F32)
        dropped = (is_dead > 0.5) & (count < DROP - 0.5)
        key = jnp.where(dropped, -1.0, tile - jnp.minimum(count, float(DROP)))
        pick = jnp.where(slot == key, 1.0, 0.0).astype(BF16)
        part = amp_ref[:, q * lanes * TW : (q + 1) * lanes * TW]
        tiles = part.astype(F32).reshape(lanes, TW).astype(BF16)
        packed = dot(pick, tiles).astype(BF16)
        for i in range(16):
            z, y = q * 4 + i // NY, i % NY
            out_ref[y * NZ + z] = packed[i * CT : i * CT + CAP, :]


def pack(me, live, amplitudes):
    return pl.pallas_call(
        pack_kernel,
        out_shape=jax.ShapeDtypeStruct((NW, CAP, TW), BF16),
        grid_spec=pltpu.PrefetchScalarGridSpec(
            num_scalar_prefetch=1,
            grid=(1,),
            in_specs=[
                pl.BlockSpec((8, NW * CT), lambda i, me: (me[0] // 8, 0)),
                pl.BlockSpec((1, NW * CT * TW), lambda i, me: (0, 0)),
            ],
            out_specs=pl.BlockSpec((NW, CAP, TW), lambda i, me: (0, 0, 0)),
        ),
        name="pack",
    )(me, live, amplitudes)


def whole(*dims):
    return pl.BlockSpec(dims, lambda i, *ids: (0,) * len(dims))


def codes_kernel(ids_ref, live_ref, out_ref):
    wide, core = ids_ref[0], ids_ref[1]
    rows = NX * NW
    r, g = iota((rows, 512), 0), iota((rows, 512), 1)
    rx, ry, rz = r // NW, (r // NZ) % NY, r % NZ
    source = ((rz * NY + ry) * NX + rx) * NC + core
    pick = jnp.where(g == source, 1.0, 0.0).astype(BF16)
    live = dot(pick, live_ref[...].astype(F32).astype(BF16)).astype(BF16)
    base = (wide % 8) * CT
    lane, c = iota((TW, TW), 0), iota((TW, TW), 1)
    take = jnp.where((lane == base + c) & (c < CT), 1.0, 0.0).astype(BF16)
    prior = jnp.where((lane >= base) & (lane < base + c) & (c < CT), 1.0, 0.0).astype(BF16)
    here = dot(live, take)
    count = dot((1.0 - live.astype(F32)).astype(BF16), prior)
    code = jnp.where(here > 0.5, jnp.minimum(count, float(DROP)), 9.0).astype(BF16)
    spread_row, spread_col = iota((TW, CT * TW), 0), iota((TW, CT * TW), 1)
    spread = jnp.where(spread_row == spread_col // TW, 1.0, 0.0).astype(BF16)
    out_ref[...] = dot(code, spread).astype(BF16)


def codes_of(ids, live):
    return pl.pallas_call(
        codes_kernel,
        out_shape=jax.ShapeDtypeStruct((NX * NW, CT * TW), BF16),
        grid_spec=pltpu.PrefetchScalarGridSpec(
            num_scalar_prefetch=1,
            grid=(1,),
            in_specs=[pl.BlockSpec((512, TW), lambda i, ids: (0, ids[0] // 8))],
            out_specs=whole(NX * NW, CT * TW),
        ),
        name="codes",
    )(ids, live)


def ladder_kernel(ids_ref, code_ref, amp_ref, own_ref, other_ref, out_ref, used_ref):
    core = ids_ref[1]
    rows = NX * NW
    for t in range(CT):
        code_t = code_ref[:, t * TW : (t + 1) * TW]
        value = jnp.zeros((rows, TW), BF16)
        for d in range(DROP + 1):
            if 0 <= t - d < CAP:
                value = jnp.where(code_t == d, amp_ref[t - d], value)
        used_ref[:, t * TW : (t + 1) * TW] = value
    used = used_ref[...]
    for ref, column in ((own_ref, core), (other_ref, 1 - core)):
        sums = lax.dot_general(used, ref[...], (((1,), (1,)), ((), ())), preferred_element_type=F32)
        for y in range(NY):
            for x in range(NX):
                at = x * NW + y * NZ
                out_ref[y, column, x * NZ : (x + 1) * NZ, :] = sums[at : at + NZ, :]


def ladder(ids, codes, amp, own, other):
    return pl.pallas_call(
        ladder_kernel,
        out_shape=jax.ShapeDtypeStruct((NY, NC, NX * NZ, 256), F32),
        grid_spec=pltpu.PrefetchScalarGridSpec(
            num_scalar_prefetch=1,
            grid=(1,),
            in_specs=[
                whole(NX * NW, CT * TW),
                whole(CAP, NX * NW, TW),
                whole(256, CT * TW),
                whole(256, CT * TW),
            ],
            out_specs=whole(NY, NC, NX * NZ, 256),
            scratch_shapes=[pltpu.VMEM((NX * NW, CT * TW), BF16)],
        ),
        compiler_params=pltpu.CompilerParams(vmem_limit_bytes=40 * 1024 * 1024),
        name="ladder",
    )(ids, codes, amp, own, other)


def finish_kernel(sums_ref, out_ref):
    for x in range(NX):
        total = jnp.sum(sums_ref[x * NZ : (x + 1) * NZ], axis=0).astype(BF16)
        for c in range(NC):
            at = (x * NC + c) * 256
            out_ref[:, at : at + 256] = total[c : c + 1, :]


def finish(sums):
    return pl.pallas_call(
        finish_kernel,
        out_shape=jax.ShapeDtypeStruct((1, NX * NC * 256), BF16),
        name="finish",
    )(sums)


def per_device(amplitudes, amplitude_live, integrals, integral_live):
    wide = lax.axis_index("z") * NY + lax.axis_index("y")
    core = lax.axis_index("c")
    me = (wide * NX + lax.axis_index("x")) * NC + core
    mask = integral_live.astype(BF16)
    own = (integrals.reshape(2, TW, CT, TW) * mask[:, None, :, None]).reshape(2 * TW, CT * TW)
    other = lax.ppermute(own, "c", [(0, 1), (1, 0)])
    packed = pack(me.reshape(1), amplitude_live, amplitudes)
    arrived = lax.all_to_all(packed, ("y", "z"), 0, 0, tiled=True)
    gathered = lax.all_gather(arrived.transpose(1, 0, 2), "x", axis=1, tiled=True)
    ids = jnp.stack([wide, core])
    sums = ladder(ids, codes_of(ids, amplitude_live), gathered, own, other)
    sums = lax.all_to_all(sums, "y", 0, 0, tiled=True).sum(axis=0)
    sums = lax.all_to_all(sums.transpose(1, 0, 2), ("x", "z"), 0, 0, tiled=True)
    return finish(sums)


def solution(mesh):
    fine = Mesh(mesh.devices.reshape(NZ, NY, NX, NC), ("z", "y", "x", "c"))
    wide, grp = ("z", "y"), ("x", "c")
    return jax.shard_map(
        per_device,
        mesh=fine,
        in_specs=(P(wide + grp, None), P(), P(grp, wide), P(grp, wide)),
        out_specs=P(wide + grp, None),
        check_vma=False,
    )
```

```python
import functools

import jax
import jax.numpy as jnp
from jax import lax
from jax.experimental import pallas as pl
from jax.experimental.pallas import tpu as pltpu
from jax.sharding import Mesh, PartitionSpec as P

TW = 128
NZ, NY, NX, NC = 16, 4, 4, 2
NW = NZ * NY
CT = 16
CAP = 12
DROP = CT - CAP
F32 = jnp.float32
BF16 = jnp.bfloat16


def iota(shape, dim):
    return lax.broadcasted_iota(jnp.int32, shape, dim)


def dot(a, b):
    return lax.dot_general(a, b, (((1,), (0,)), ((), ())), preferred_element_type=F32)


def before_matrix():
    rows, cols = iota((TW, TW), 0), iota((TW, TW), 1)
    same = (rows // CT) == (cols // CT)
    return jnp.where(same & (rows < cols), 1.0, 0.0).astype(BF16)


def pack_kernel(me_ref, live_ref, amp_ref, out_ref):
    sub = me_ref[0] % 8
    live = live_ref[...].astype(F32)
    row = jnp.sum(jnp.where(iota(live.shape, 0) == sub, live, 0.0), axis=0, keepdims=True)
    dead = jnp.broadcast_to(1.0 - row, (8, NW * CT)).astype(BF16)
    before = before_matrix()
    lanes = 2 * TW
    out_row, col = iota((lanes, lanes), 0), iota((lanes, lanes), 1)
    slot = jnp.where(out_row // CT == col // CT, out_row % CT, -7).astype(F32)
    tile = (iota((1, lanes), 1) % CT).astype(F32)
    for q in range(4):
        dead_q = dead[:, q * lanes : (q + 1) * lanes]
        count = jnp.concatenate([dot(dead_q[:, :TW], before), dot(dead_q[:, TW:], before)], axis=1)[0:1]
        dropped = (row[:, q * lanes : (q + 1) * lanes] < 0.5) & (count < DROP - 0.5)
        key = jnp.where(dropped, -1.0, tile - jnp.minimum(count, float(DROP)))
        pick = jnp.where(slot == key, 1.0, 0.0).astype(BF16)
        part = amp_ref[:, q * lanes * TW : (q + 1) * lanes * TW]
        tiles = part.astype(F32).reshape(lanes, TW).astype(BF16)
        packed = dot(pick, tiles).astype(BF16)
        for i in range(16):
            z, y = q * 4 + i // NY, i % NY
            for k in range(CAP // 4):
                at = i * CT + k * 4
                out_ref[y * NZ + z, :, k * TW : (k + 1) * TW] = packed[at : at + 4, :]


def pack(me, live, amplitudes):
    return pl.pallas_call(
        pack_kernel,
        out_shape=jax.ShapeDtypeStruct((NW, 4, CAP // 4 * TW), BF16),
        grid_spec=pltpu.PrefetchScalarGridSpec(
            num_scalar_prefetch=1,
            grid=(1,),
            in_specs=[
                pl.BlockSpec((8, NW * CT), lambda i, me: (me[0] // 8, 0)),
                pl.BlockSpec((1, NW * CT * TW), lambda i, me: (0, 0)),
            ],
            out_specs=pl.BlockSpec((NW, 4, CAP // 4 * TW), lambda i, me: (0, 0, 0)),
        ),
        name="pack",
    )(me, live, amplitudes)


def whole(*dims):
    return pl.BlockSpec(dims, lambda i, *ids: (0,) * len(dims))


def codes_kernel(ids_ref, live_ref, out_ref):
    wide, core = ids_ref[0], ids_ref[1]
    rows = NX * NW
    r, g = iota((rows, 512), 0), iota((rows, 512), 1)
    rx, ry, rz = r // NW, (r // NZ) % NY, r % NZ
    source = ((rz * NY + ry) * NX + rx) * NC + core
    pick = jnp.where(g == source, 1.0, 0.0).astype(BF16)
    live = dot(pick, live_ref[...].astype(F32).astype(BF16)).astype(BF16)
    base = (wide % 8) * CT
    lane, c = iota((TW, TW), 0), iota((TW, TW), 1)
    take = jnp.where((lane == base + c) & (c < CT), 1.0, 0.0).astype(BF16)
    prior = jnp.where((lane >= base) & (lane < base + c) & (c < CT), 1.0, 0.0).astype(BF16)
    here = dot(live, take)
    count = dot((1.0 - live.astype(F32)).astype(BF16), prior)
    code = jnp.where(here > 0.5, jnp.minimum(count, float(DROP)), 9.0).astype(BF16)
    spread_row, spread_col = iota((TW, CT * TW), 0), iota((TW, CT * TW), 1)
    spread = jnp.where(spread_row == spread_col // TW, 1.0, 0.0).astype(BF16)
    out_ref[...] = dot(code, spread).astype(BF16)


def codes_of(ids, live):
    return pl.pallas_call(
        codes_kernel,
        out_shape=jax.ShapeDtypeStruct((NX * NW, CT * TW), BF16),
        grid_spec=pltpu.PrefetchScalarGridSpec(
            num_scalar_prefetch=1,
            grid=(1,),
            in_specs=[pl.BlockSpec((512, TW), lambda i, ids: (0, ids[0] // 8))],
            out_specs=whole(NX * NW, CT * TW),
        ),
        name="codes",
    )(ids, live)


def ladder_kernel(ids_ref, code_ref, amp_ref, own_ref, other_ref, out_ref, used_ref):
    core = ids_ref[1]
    rows = NX * NW
    slots = [amp_ref[j % 4, :, j // 4 * TW : (j // 4 + 1) * TW] for j in range(CAP)]
    for t in range(CT):
        code_t = code_ref[:, t * TW : (t + 1) * TW]
        value = jnp.zeros((rows, TW), BF16)
        for d in range(DROP + 1):
            if 0 <= t - d < CAP:
                value = jnp.where(code_t == d, slots[t - d], value)
        used_ref[:, t * TW : (t + 1) * TW] = value
    used = used_ref[...]
    for ref, column in ((own_ref, core), (other_ref, 1 - core)):
        sums = lax.dot_general(used, ref[...], (((1,), (1,)), ((), ())), preferred_element_type=F32)
        for y in range(NY):
            for x in range(NX):
                at = x * NW + y * NZ
                out_ref[y * NX + x, column] = sums[at : at + NZ, :]


def ladder(ids, codes, amp, own, other):
    return pl.pallas_call(
        ladder_kernel,
        out_shape=jax.ShapeDtypeStruct((NY * NX, NC, NZ, 256), F32),
        grid_spec=pltpu.PrefetchScalarGridSpec(
            num_scalar_prefetch=1,
            grid=(1,),
            in_specs=[
                whole(NX * NW, CT * TW),
                whole(4, NX * NW, CAP // 4 * TW),
                whole(256, CT * TW),
                whole(256, CT * TW),
            ],
            out_specs=whole(NY * NX, NC, NZ, 256),
            scratch_shapes=[pltpu.VMEM((NX * NW, CT * TW), BF16)],
        ),
        compiler_params=pltpu.CompilerParams(vmem_limit_bytes=40 * 1024 * 1024),
        name="ladder",
    )(ids, codes, amp, own, other)


def per_device(amplitudes, amplitude_live, integrals, integral_live):
    wide = lax.axis_index("z") * NY + lax.axis_index("y")
    core = lax.axis_index("c")
    me = (wide * NX + lax.axis_index("x")) * NC + core
    mask = integral_live.astype(BF16)
    own = (integrals.reshape(2, TW, CT, TW) * mask[:, None, :, None]).reshape(2 * TW, CT * TW)
    other = lax.ppermute(own, "c", [(0, 1), (1, 0)])
    packed = pack(me.reshape(1), amplitude_live, amplitudes)
    arrived = lax.all_to_all(packed, ("y", "z"), 0, 0, tiled=True)
    slots = arrived.transpose(1, 0, 2)
    gathered = lax.all_gather(slots, "x", axis=1, tiled=True)
    ids = jnp.stack([wide, core])
    sums = ladder(ids, codes_of(ids, amplitude_live), gathered, own, other)
    sums = lax.all_to_all(sums, ("y", "x"), 0, 0, tiled=True)
    sums = sums.reshape(NY, NX, NC, NZ, 256).sum(axis=0)
    sums = sums.transpose(2, 0, 1, 3).reshape(NZ, 16, TW)
    sums = lax.all_to_all(sums, "z", 0, 0, tiled=True).sum(axis=0)
    return sums.astype(BF16).reshape(1, NX * NC * 256)


def solution(mesh):
    fine = Mesh(mesh.devices.reshape(NZ, NY, NX, NC), ("z", "y", "x", "c"))
    wide, grp = ("z", "y"), ("x", "c")
    return jax.shard_map(
        per_device,
        mesh=fine,
        in_specs=(P(wide + grp, None), P(), P(grp, wide), P(grp, wide)),
        out_specs=P(wide + grp, None),
        check_vma=False,
    )
```

```python
import functools

import jax
import jax.numpy as jnp
from jax import lax
from jax.experimental import pallas as pl
from jax.experimental.pallas import tpu as pltpu
from jax.sharding import Mesh, PartitionSpec as P

TW = 128
NZ, NY, NX, NC = 16, 4, 4, 2
NW = NZ * NY
CT = 16
CAP = 12
DROP = CT - CAP
F32 = jnp.float32
BF16 = jnp.bfloat16


def iota(shape, dim):
    return lax.broadcasted_iota(jnp.int32, shape, dim)


def dot(a, b):
    return lax.dot_general(a, b, (((1,), (0,)), ((), ())), preferred_element_type=F32)


def before_matrix():
    rows, cols = iota((TW, TW), 0), iota((TW, TW), 1)
    same = (rows >> 4) == (cols >> 4)
    return jnp.where(same & (rows < cols), 1.0, 0.0).astype(BF16)


def own_wide():
    return lax.axis_index("z") * NY + lax.axis_index("y")


def pack_kernel(live_ref, amp_ref, out_ref, live_in, amp_in, packed_out, live_sem, in_sem, out_sem):
    lanes = 2 * TW
    block = pl.multiple_of(own_wide() * 8, 8)
    fetch_live = pltpu.make_async_copy(live_ref.at[pl.ds(block, 8)], live_in, live_sem)
    fetch_live.start()
    fetch = [
        pltpu.make_async_copy(amp_ref.at[:, pl.ds(q * lanes * TW, lanes * TW)], amp_in.at[q], in_sem.at[q])
        for q in range(4)
    ]
    for copy in fetch:
        copy.start()
    before = before_matrix()
    out_row, col = iota((lanes, lanes), 0), iota((lanes, lanes), 1)
    slot = jnp.where(out_row >> 4 == col >> 4, out_row & 15, -7).astype(F32)
    tile = (iota((1, lanes), 1) & 15).astype(F32)
    fetch_live.wait()
    live = live_in[...].astype(F32)
    sub = lax.axis_index("x") * NC + lax.axis_index("c")
    row = jnp.sum(jnp.where(iota(live.shape, 0) == sub, live, 0.0), axis=0, keepdims=True)
    dead = jnp.broadcast_to(1.0 - row, (8, NW * CT)).astype(BF16)
    blocks = jnp.concatenate([dead[:, j * TW : (j + 1) * TW] for j in range(8)], axis=0)
    counts = dot(blocks, before)
    picks = []
    for q in range(4):
        count = jnp.concatenate([counts[16 * q : 16 * q + 1], counts[16 * q + 8 : 16 * q + 9]], axis=1)
        dropped = (row[:, q * lanes : (q + 1) * lanes] < 0.5) & (count < DROP - 0.5)
        key = jnp.where(dropped, -1.0, tile - jnp.minimum(count, float(DROP)))
        picks.append(jnp.where(slot == key, 1.0, 0.0).astype(BF16))
    for copy in fetch:
        copy.wait()
    tiles = [amp_in[q].astype(F32).reshape(lanes, TW).astype(BF16) for q in range(4)]
    packs = [dot(picks[q], tiles[q]).astype(BF16) for q in range(4)]
    store = []
    for q in range(4):
        for i in range(16):
            for k in range(CAP // 4):
                at = i * CT + k * 4
                packed_out[q, i, :, k * TW : (k + 1) * TW] = packs[q][at : at + 4, :]
        copy = pltpu.make_async_copy(packed_out.at[q], out_ref.at[pl.ds(q * 16, 16)], out_sem.at[q])
        copy.start()
        store.append(copy)
    for copy in store:
        copy.wait()


def pack(live, amplitudes):
    lanes = 2 * TW
    anywhere = pl.BlockSpec(memory_space=pl.ANY)
    return pl.pallas_call(
        pack_kernel,
        out_shape=jax.ShapeDtypeStruct((NW, 4, CAP // 4 * TW), BF16),
        in_specs=[anywhere, anywhere],
        out_specs=anywhere,
        scratch_shapes=[
            pltpu.VMEM((8, NW * CT), jnp.int32),
            pltpu.VMEM((4, 1, lanes * TW), BF16),
            pltpu.VMEM((4, 16, 4, CAP // 4 * TW), BF16),
            pltpu.SemaphoreType.DMA,
            pltpu.SemaphoreType.DMA((4,)),
            pltpu.SemaphoreType.DMA((4,)),
        ],
        name="pack",
    )(live, amplitudes)


def whole(*dims):
    return pl.BlockSpec(dims, lambda i, *ids: (0,) * len(dims))


def codes_kernel(ids_ref, live_ref, out_ref):
    wide, core = ids_ref[0], ids_ref[1]
    rows = NX * NW
    r, g = iota((rows, 512), 0), iota((rows, 512), 1)
    rx, ry, rz = r >> 6, (r >> 4) & 3, r & 15
    source = (rz << 5) + (ry << 3) + (rx << 1) + core
    pick = jnp.where(g == source, 1.0, 0.0).astype(BF16)
    live = dot(pick, live_ref[...].astype(F32).astype(BF16)).astype(BF16)
    base = (wide % 8) * CT
    lane, c = iota((TW, TW), 0), iota((TW, TW), 1)
    take = jnp.where((lane == base + c) & (c < CT), 1.0, 0.0).astype(BF16)
    prior = jnp.where((lane >= base) & (lane < base + c) & (c < CT), 1.0, 0.0).astype(BF16)
    here = dot(live, take)
    count = dot((1.0 - live.astype(F32)).astype(BF16), prior)
    code = jnp.where(here > 0.5, jnp.minimum(count, float(DROP)), 9.0).astype(BF16)
    spread_row, spread_col = iota((TW, CT * TW), 0), iota((TW, CT * TW), 1)
    spread = jnp.where(spread_row == spread_col // TW, 1.0, 0.0).astype(BF16)
    out_ref[...] = dot(code, spread).astype(BF16)


def codes_of(ids, live):
    return pl.pallas_call(
        codes_kernel,
        out_shape=jax.ShapeDtypeStruct((NX * NW, CT * TW), BF16),
        grid_spec=pltpu.PrefetchScalarGridSpec(
            num_scalar_prefetch=1,
            grid=(1,),
            in_specs=[pl.BlockSpec((512, TW), lambda i, ids: (0, ids[0] // 8))],
            out_specs=whole(NX * NW, CT * TW),
        ),
        name="codes",
    )(ids, live)


def ladder_kernel(code_ref, amp_ref, own_ref, other_ref, out_ref, used_ref):
    core = lax.axis_index("c")
    rows = NX * NW
    slots = [amp_ref[j % 4, :, j // 4 * TW : (j // 4 + 1) * TW] for j in range(CAP)]
    for t in range(CT):
        code_t = code_ref[:, t * TW : (t + 1) * TW]
        value = jnp.zeros((rows, TW), BF16)
        for d in range(DROP + 1):
            if 0 <= t - d < CAP:
                value = jnp.where(code_t == d, slots[t - d], value)
        used_ref[:, t * TW : (t + 1) * TW] = value
    used = used_ref[...]
    for ref, column in ((own_ref, core), (other_ref, 1 - core)):
        sums = lax.dot_general(used, ref[...], (((1,), (1,)), ((), ())), preferred_element_type=F32)
        for i in range(NX * NY):
            out_ref[i, column] = sums[i * NZ : (i + 1) * NZ, :]


def ladder(codes, amp, own, other):
    return pl.pallas_call(
        ladder_kernel,
        out_shape=jax.ShapeDtypeStruct((NY * NX, NC, NZ, 256), F32),
        scratch_shapes=[pltpu.VMEM((NX * NW, CT * TW), BF16)],
        compiler_params=pltpu.CompilerParams(vmem_limit_bytes=40 * 1024 * 1024),
        name="ladder",
    )(codes, amp, own, other)


def per_device(amplitudes, amplitude_live, integrals, integral_live):
    mask = integral_live.astype(BF16)
    own = (integrals.reshape(2, TW, CT, TW) * mask[:, None, :, None]).reshape(2 * TW, CT * TW)
    other = lax.ppermute(own, "c", [(0, 1), (1, 0)])
    packed = pack(amplitude_live, amplitudes)
    arrived = lax.all_to_all(packed, ("z", "y"), 0, 0, tiled=True)
    slots = arrived.reshape(NZ, NY, 4, CAP // 4 * TW).transpose(2, 1, 0, 3).reshape(4, NW, CAP // 4 * TW)
    gathered = lax.all_gather(slots, "x", axis=1, tiled=True)
    ids = jnp.stack([own_wide(), lax.axis_index("c")])
    sums = ladder(codes_of(ids, amplitude_live), gathered, own, other)
    sums = lax.all_to_all(sums, ("x", "y"), 0, 0, tiled=True)
    sums = sums.reshape(NX, NY, NC, NZ, 256).sum(axis=1)
    sums = sums.transpose(2, 0, 1, 3).reshape(NZ, 16, TW)
    sums = lax.all_to_all(sums, "z", 0, 0, tiled=True).sum(axis=0)
    return sums.astype(BF16).reshape(1, NX * NC * 256)


def solution(mesh):
    fine = Mesh(mesh.devices.reshape(NZ, NY, NX, NC), ("z", "y", "x", "c"))
    wide, grp = ("z", "y"), ("x", "c")
    return jax.shard_map(
        per_device,
        mesh=fine,
        in_specs=(P(wide + grp, None), P(), P(grp, wide), P(grp, wide)),
        out_specs=P(wide + grp, None),
        check_vma=False,
    )
```

```python
import functools

import jax
import jax.numpy as jnp
from jax import lax
from jax.experimental import pallas as pl
from jax.experimental.pallas import tpu as pltpu
from jax.sharding import Mesh, PartitionSpec as P

TW = 128
NZ, NY, NX, NC = 16, 4, 4, 2
NW = NZ * NY
CT = 16
CAP = 12
DROP = CT - CAP
F32 = jnp.float32
BF16 = jnp.bfloat16


def iota(shape, dim):
    return lax.broadcasted_iota(jnp.int32, shape, dim)


def dot(a, b):
    return lax.dot_general(a, b, (((1,), (0,)), ((), ())), preferred_element_type=F32)


def before_matrix():
    rows, cols = iota((TW, TW), 0), iota((TW, TW), 1)
    same = (rows >> 4) == (cols >> 4)
    return jnp.where(same & (rows < cols), 1.0, 0.0).astype(BF16)


def own_wide():
    return lax.axis_index("z") * NY + lax.axis_index("y")


def pack_kernel(live_ref, amp_ref, out_ref, live_in, amp_in, packed_out, live_sem, amp_sem, out_sem):
    lanes = 2 * TW
    block = pl.multiple_of(own_wide() * 8, 8)
    fetch_live = pltpu.make_async_copy(live_ref.at[pl.ds(block, 8)], live_in, live_sem)
    fetch_live.start()
    fetch_amp = pltpu.make_async_copy(amp_ref, amp_in, amp_sem)
    fetch_amp.start()
    before = before_matrix()
    out_row, col = iota((lanes, lanes), 0), iota((lanes, lanes), 1)
    slot = jnp.where(out_row >> 4 == col >> 4, out_row & 15, -7).astype(F32)
    tile = (iota((1, lanes), 1) & 15).astype(F32)
    fetch_live.wait()
    live = live_in[...].astype(F32)
    sub = lax.axis_index("x") * NC + lax.axis_index("c")
    row = jnp.sum(jnp.where(iota(live.shape, 0) == sub, live, 0.0), axis=0, keepdims=True)
    dead = jnp.broadcast_to(1.0 - row, (8, NW * CT)).astype(BF16)
    blocks = jnp.concatenate([dead[:, j * TW : (j + 1) * TW] for j in range(8)], axis=0)
    counts = dot(blocks, before)
    picks = []
    for q in range(4):
        count = jnp.concatenate([counts[16 * q : 16 * q + 1], counts[16 * q + 8 : 16 * q + 9]], axis=1)
        dropped = (row[:, q * lanes : (q + 1) * lanes] < 0.5) & (count < DROP - 0.5)
        key = jnp.where(dropped, -1.0, tile - jnp.minimum(count, float(DROP)))
        picks.append(jnp.where(slot == key, 1.0, 0.0).astype(BF16))
    fetch_amp.wait()
    tiles = [amp_in[:, q * lanes * TW : (q + 1) * lanes * TW].astype(F32).reshape(lanes, TW).astype(BF16) for q in range(4)]
    packs = [dot(picks[q], tiles[q]).astype(BF16) for q in range(4)]
    store = []
    for q in range(4):
        for i in range(16):
            for k in range(CAP // 4):
                at = i * CT + k * 4
                packed_out[q, i, :, k * TW : (k + 1) * TW] = packs[q][at : at + 4, :]
        copy = pltpu.make_async_copy(packed_out.at[q], out_ref.at[pl.ds(q * 16, 16)], out_sem.at[q])
        copy.start()
        store.append(copy)
    for copy in store:
        copy.wait()


def pack(live, amplitudes):
    lanes = 2 * TW
    anywhere = pl.BlockSpec(memory_space=pl.ANY)
    return pl.pallas_call(
        pack_kernel,
        out_shape=jax.ShapeDtypeStruct((NW, 4, CAP // 4 * TW), BF16),
        in_specs=[anywhere, anywhere],
        out_specs=anywhere,
        scratch_shapes=[
            pltpu.VMEM((8, NW * CT), jnp.int32),
            pltpu.VMEM((1, NW * CT * TW), BF16),
            pltpu.VMEM((4, 16, 4, CAP // 4 * TW), BF16),
            pltpu.SemaphoreType.DMA,
            pltpu.SemaphoreType.DMA,
            pltpu.SemaphoreType.DMA((4,)),
        ],
        name="pack",
    )(live, amplitudes)


def whole(*dims):
    return pl.BlockSpec(dims, lambda i, *ids: (0,) * len(dims))


def codes_kernel(ids_ref, live_ref, out_ref):
    wide, core = ids_ref[0], ids_ref[1]
    rows = NX * NW
    r, g = iota((rows, 512), 0), iota((rows, 512), 1)
    rx, ry, rz = r >> 6, (r >> 4) & 3, r & 15
    source = (rz << 5) + (ry << 3) + (rx << 1) + core
    pick = jnp.where(g == source, 1.0, 0.0).astype(BF16)
    live = dot(pick, live_ref[...].astype(F32).astype(BF16)).astype(BF16)
    base = (wide % 8) * CT
    lane, c = iota((TW, TW), 0), iota((TW, TW), 1)
    take = jnp.where((lane == base + c) & (c < CT), 1.0, 0.0).astype(BF16)
    prior = jnp.where((lane >= base) & (lane < base + c) & (c < CT), 1.0, 0.0).astype(BF16)
    here = dot(live, take)
    count = dot((1.0 - live.astype(F32)).astype(BF16), prior)
    code = jnp.where(here > 0.5, jnp.minimum(count, float(DROP)), 9.0).astype(BF16)
    spread_row, spread_col = iota((TW, CT * TW), 0), iota((TW, CT * TW), 1)
    spread = jnp.where(spread_row == spread_col // TW, 1.0, 0.0).astype(BF16)
    out_ref[...] = dot(code, spread).astype(BF16)


def codes_of(ids, live):
    return pl.pallas_call(
        codes_kernel,
        out_shape=jax.ShapeDtypeStruct((NX * NW, CT * TW), BF16),
        grid_spec=pltpu.PrefetchScalarGridSpec(
            num_scalar_prefetch=1,
            grid=(1,),
            in_specs=[pl.BlockSpec((512, TW), lambda i, ids: (0, ids[0] // 8))],
            out_specs=whole(NX * NW, CT * TW),
        ),
        name="codes",
    )(ids, live)


def ladder_kernel(code_ref, amp_ref, own_ref, other_ref, out_ref, used_ref):
    core = lax.axis_index("c")
    rows = NX * NW
    slots = [
        jnp.concatenate([amp_ref[x * 4 + j % 4, :, j // 4 * TW : (j // 4 + 1) * TW] for x in range(NX)])
        for j in range(CAP)
    ]
    for t in range(CT):
        code_t = code_ref[:, t * TW : (t + 1) * TW]
        value = jnp.zeros((rows, TW), BF16)
        for d in range(DROP + 1):
            if 0 <= t - d < CAP:
                value = jnp.where(code_t == d, slots[t - d], value)
        used_ref[:, t * TW : (t + 1) * TW] = value
    used = used_ref[...]
    for ref, column in ((own_ref, core), (other_ref, 1 - core)):
        sums = lax.dot_general(used, ref[...], (((1,), (1,)), ((), ())), preferred_element_type=F32)
        for i in range(NX * NY):
            out_ref[i, column] = sums[i * NZ : (i + 1) * NZ, :]


def ladder(codes, amp, own, other):
    return pl.pallas_call(
        ladder_kernel,
        out_shape=jax.ShapeDtypeStruct((NY * NX, NC, NZ, 256), F32),
        scratch_shapes=[pltpu.VMEM((NX * NW, CT * TW), BF16)],
        compiler_params=pltpu.CompilerParams(vmem_limit_bytes=40 * 1024 * 1024),
        name="ladder",
    )(codes, amp, own, other)


def per_device(amplitudes, amplitude_live, integrals, integral_live):
    mask = integral_live.astype(BF16)
    own = (integrals.reshape(2, TW, CT, TW) * mask[:, None, :, None]).reshape(2 * TW, CT * TW)
    other = lax.ppermute(own, "c", [(0, 1), (1, 0)])
    packed = pack(amplitude_live, amplitudes)
    arrived = lax.all_to_all(packed, ("z", "y"), 0, 0, tiled=True)
    slots = arrived.reshape(NZ, NY, 4, CAP // 4 * TW).transpose(2, 1, 0, 3).reshape(4, NW, CAP // 4 * TW)
    gathered = lax.all_gather(slots, "x", axis=0, tiled=True)
    ids = jnp.stack([own_wide(), lax.axis_index("c")])
    sums = ladder(codes_of(ids, amplitude_live), gathered, own, other)
    sums = lax.all_to_all(sums, ("x", "y"), 0, 0, tiled=True)
    sums = sums.reshape(NX, NY, NC, NZ, 256).sum(axis=1)
    sums = sums.transpose(2, 0, 1, 3).reshape(NZ, 16, TW)
    sums = lax.all_to_all(sums, "z", 0, 0, tiled=True).sum(axis=0)
    sums = lax.optimization_barrier(sums.reshape(1, NX * NC * 256))
    return sums.astype(BF16)


def solution(mesh):
    fine = Mesh(mesh.devices.reshape(NZ, NY, NX, NC), ("z", "y", "x", "c"))
    wide, grp = ("z", "y"), ("x", "c")
    return jax.shard_map(
        per_device,
        mesh=fine,
        in_specs=(P(wide + grp, None), P(), P(grp, wide), P(grp, wide)),
        out_specs=P(wide + grp, None),
        check_vma=False,
    )
```

```python
import functools

import jax
import jax.numpy as jnp
from jax import lax
from jax.experimental import pallas as pl
from jax.experimental.pallas import tpu as pltpu
from jax.sharding import Mesh, PartitionSpec as P

TW = 128
NZ, NY, NX, NC = 16, 4, 4, 2
NW = NZ * NY
CT = 16
CAP = 12
DROP = CT - CAP
F32 = jnp.float32
BF16 = jnp.bfloat16


def iota(shape, dim):
    return lax.broadcasted_iota(jnp.int32, shape, dim)


def dot(a, b):
    return lax.dot_general(a, b, (((1,), (0,)), ((), ())), preferred_element_type=F32)


def before_matrix():
    rows, cols = iota((TW, TW), 0), iota((TW, TW), 1)
    same = (rows >> 4) == (cols >> 4)
    return jnp.where(same & (rows < cols), 1.0, 0.0).astype(BF16)


def own_wide():
    return lax.axis_index("z") * NY + lax.axis_index("y")


def pack_kernel(live_ref, amp_ref, out_ref, live_in, amp_in, packed_out, live_sem, amp_sem, out_sem):
    lanes = 2 * TW
    block = pl.multiple_of(own_wide() * 8, 8)
    fetch_live = pltpu.make_async_copy(live_ref.at[pl.ds(block, 8)], live_in, live_sem)
    fetch_live.start()
    fetch_amp = pltpu.make_async_copy(amp_ref, amp_in, amp_sem)
    fetch_amp.start()
    before = before_matrix()
    out_row, col = iota((lanes, lanes), 0), iota((lanes, lanes), 1)
    slot = jnp.where(out_row >> 4 == col >> 4, out_row & 15, -7).astype(F32)
    tile = (iota((1, lanes), 1) & 15).astype(F32)
    fetch_live.wait()
    live = live_in[...].astype(F32)
    sub = lax.axis_index("x") * NC + lax.axis_index("c")
    row = jnp.sum(jnp.where(iota(live.shape, 0) == sub, live, 0.0), axis=0, keepdims=True)
    dead = jnp.broadcast_to(1.0 - row, (8, NW * CT)).astype(BF16)
    blocks = jnp.concatenate([dead[:, j * TW : (j + 1) * TW] for j in range(8)], axis=0)
    counts = dot(blocks, before)
    picks = []
    for q in range(4):
        count = jnp.concatenate([counts[16 * q : 16 * q + 1], counts[16 * q + 8 : 16 * q + 9]], axis=1)
        dropped = (row[:, q * lanes : (q + 1) * lanes] < 0.5) & (count < DROP - 0.5)
        key = jnp.where(dropped, -1.0, tile - jnp.minimum(count, float(DROP)))
        picks.append(jnp.where(slot == key, 1.0, 0.0).astype(BF16))
    fetch_amp.wait()
    tiles = [amp_in[:, q * lanes * TW : (q + 1) * lanes * TW].astype(F32).reshape(lanes, TW).astype(BF16) for q in range(4)]
    packs = [dot(picks[q], tiles[q]).astype(BF16) for q in range(4)]
    for q in range(4):
        for i in range(16):
            for k in range(CAP // 4):
                at = i * CT + k * 4
                packed_out[q * 16 + i, :, k * TW : (k + 1) * TW] = packs[q][at : at + 4, :]
    store = pltpu.make_async_copy(packed_out, out_ref, out_sem)
    store.start()
    store.wait()


def pack(live, amplitudes):
    lanes = 2 * TW
    anywhere = pl.BlockSpec(memory_space=pl.ANY)
    return pl.pallas_call(
        pack_kernel,
        out_shape=jax.ShapeDtypeStruct((NW, 4, CAP // 4 * TW), BF16),
        in_specs=[anywhere, anywhere],
        out_specs=anywhere,
        scratch_shapes=[
            pltpu.VMEM((8, NW * CT), jnp.int32),
            pltpu.VMEM((1, NW * CT * TW), BF16),
            pltpu.VMEM((NW, 4, CAP // 4 * TW), BF16),
            pltpu.SemaphoreType.DMA,
            pltpu.SemaphoreType.DMA,
            pltpu.SemaphoreType.DMA,
        ],
        name="pack",
    )(live, amplitudes)


def whole(*dims):
    return pl.BlockSpec(dims, lambda i, *ids: (0,) * len(dims))


def codes_kernel(ids_ref, live_ref, out_ref):
    wide, core = ids_ref[0], ids_ref[1]
    rows = NX * NW
    r, g = iota((rows, 512), 0), iota((rows, 512), 1)
    rx, ry, rz = r >> 6, (r >> 4) & 3, r & 15
    source = (rz << 5) + (ry << 3) + (rx << 1) + core
    pick = jnp.where(g == source, 1.0, 0.0).astype(BF16)
    live = dot(pick, live_ref[...].astype(F32).astype(BF16)).astype(BF16)
    base = (wide % 8) * CT
    lane, c = iota((TW, TW), 0), iota((TW, TW), 1)
    take = jnp.where((lane == base + c) & (c < CT), 1.0, 0.0).astype(BF16)
    prior = jnp.where((lane >= base) & (lane < base + c) & (c < CT), 1.0, 0.0).astype(BF16)
    here = dot(live, take)
    count = dot((1.0 - live.astype(F32)).astype(BF16), prior)
    code = jnp.where(here > 0.5, jnp.minimum(count, float(DROP)), 9.0).astype(BF16)
    spread_row, spread_col = iota((TW, CT * TW), 0), iota((TW, CT * TW), 1)
    spread = jnp.where(spread_row == spread_col // TW, 1.0, 0.0).astype(BF16)
    out_ref[...] = dot(code, spread).astype(BF16)


def codes_of(ids, live):
    return pl.pallas_call(
        codes_kernel,
        out_shape=jax.ShapeDtypeStruct((NX * NW, CT * TW), BF16),
        grid_spec=pltpu.PrefetchScalarGridSpec(
            num_scalar_prefetch=1,
            grid=(1,),
            in_specs=[pl.BlockSpec((512, TW), lambda i, ids: (0, ids[0] // 8))],
            out_specs=whole(NX * NW, CT * TW),
        ),
        name="codes",
    )(ids, live)


def ladder_kernel(code_ref, amp_ref, own_ref, other_ref, out_ref):
    core = lax.axis_index("c")
    rows = NX * NW
    slots = [
        jnp.concatenate([amp_ref[x * 4 + j % 4, :, j // 4 * TW : (j // 4 + 1) * TW] for x in range(NX)])
        for j in range(CAP)
    ]
    sums = [None, None]
    for first in range(0, CT, 2):
        values = []
        for t in (first, first + 1):
            code_t = code_ref[:, t * TW : (t + 1) * TW]
            value = jnp.zeros((rows, TW), BF16)
            for d in range(DROP + 1):
                if 0 <= t - d < CAP:
                    value = jnp.where(code_t == d, slots[t - d], value)
            values.append(value)
        used = jnp.concatenate(values, axis=1)
        for i, ref in enumerate((own_ref, other_ref)):
            part = ref[:, first * TW : (first + 2) * TW]
            more = lax.dot_general(used, part, (((1,), (1,)), ((), ())), preferred_element_type=F32)
            sums[i] = more if sums[i] is None else sums[i] + more
    for total, column in ((sums[0], core), (sums[1], 1 - core)):
        for i in range(NX * NY):
            out_ref[i, column] = total[i * NZ : (i + 1) * NZ, :]


def ladder(codes, amp, own, other):
    return pl.pallas_call(
        ladder_kernel,
        out_shape=jax.ShapeDtypeStruct((NY * NX, NC, NZ, 256), F32),
        compiler_params=pltpu.CompilerParams(vmem_limit_bytes=40 * 1024 * 1024),
        name="ladder",
    )(codes, amp, own, other)


def per_device(amplitudes, amplitude_live, integrals, integral_live):
    mask = integral_live.astype(BF16)
    own = (integrals.reshape(2, TW, CT, TW) * mask[:, None, :, None]).reshape(2 * TW, CT * TW)
    other = lax.ppermute(own, "c", [(0, 1), (1, 0)])
    packed = pack(amplitude_live, amplitudes)
    arrived = lax.all_to_all(packed, ("z", "y"), 0, 0, tiled=True)
    slots = arrived.reshape(NZ, NY, 4, CAP // 4 * TW).transpose(2, 1, 0, 3).reshape(4, NW, CAP // 4 * TW)
    gathered = lax.all_gather(slots, "x", axis=0, tiled=True)
    ids = jnp.stack([own_wide(), lax.axis_index("c")])
    sums = ladder(codes_of(ids, amplitude_live), gathered, own, other)
    sums = lax.all_to_all(sums, ("x", "y"), 0, 0, tiled=True)
    sums = sums.reshape(NX, NY, NC, NZ, 256).sum(axis=1)
    sums = sums.transpose(2, 0, 1, 3).reshape(NZ, 16, TW)
    sums = lax.all_to_all(sums, "z", 0, 0, tiled=True).sum(axis=0)
    sums = lax.optimization_barrier(sums.reshape(1, NX * NC * 256))
    return sums.astype(BF16)


def solution(mesh):
    fine = Mesh(mesh.devices.reshape(NZ, NY, NX, NC), ("z", "y", "x", "c"))
    wide, grp = ("z", "y"), ("x", "c")
    return jax.shard_map(
        per_device,
        mesh=fine,
        in_specs=(P(wide + grp, None), P(), P(grp, wide), P(grp, wide)),
        out_specs=P(wide + grp, None),
        check_vma=False,
    )
```

```python
import functools

import jax
import jax.numpy as jnp
from jax import lax
from jax.experimental import pallas as pl
from jax.experimental.pallas import tpu as pltpu
from jax.sharding import Mesh, PartitionSpec as P

TW = 128
NZ, NY, NX, NC = 16, 4, 4, 2
NW = NZ * NY
CT = 16
CAP = 12
DROP = CT - CAP
F32 = jnp.float32
BF16 = jnp.bfloat16


def iota(shape, dim):
    return lax.broadcasted_iota(jnp.int32, shape, dim)


def dot(a, b):
    return lax.dot_general(a, b, (((1,), (0,)), ((), ())), preferred_element_type=F32)


def before_matrix():
    rows, cols = iota((TW, TW), 0), iota((TW, TW), 1)
    same = (rows >> 4) == (cols >> 4)
    return jnp.where(same & (rows < cols), 1.0, 0.0).astype(BF16)


def own_wide():
    return lax.axis_index("z") * NY + lax.axis_index("y")


def pack_kernel(live_ref, amp_ref, out_ref, live_in, amp_in, packed_out, live_sem, amp_sem, out_sem):
    lanes = 2 * TW
    block = pl.multiple_of(own_wide() * 8, 8)
    fetch_live = pltpu.make_async_copy(live_ref.at[pl.ds(block, 8)], live_in, live_sem)
    fetch_live.start()
    fetch_amp = pltpu.make_async_copy(amp_ref, amp_in, amp_sem)
    fetch_amp.start()
    before = before_matrix()
    out_row, col = iota((lanes, lanes), 0), iota((lanes, lanes), 1)
    slot = jnp.where(out_row >> 4 == col >> 4, out_row & 15, -7).astype(F32)
    tile = (iota((1, lanes), 1) & 15).astype(F32)
    fetch_live.wait()
    live = live_in[...].astype(F32)
    sub = lax.axis_index("x") * NC + lax.axis_index("c")
    row = jnp.sum(jnp.where(iota(live.shape, 0) == sub, live, 0.0), axis=0, keepdims=True)
    dead = jnp.broadcast_to(1.0 - row, (8, NW * CT)).astype(BF16)
    blocks = jnp.concatenate([dead[:, j * TW : (j + 1) * TW] for j in range(8)], axis=0)
    counts = dot(blocks, before)
    picks = []
    for q in range(4):
        count = jnp.concatenate([counts[16 * q : 16 * q + 1], counts[16 * q + 8 : 16 * q + 9]], axis=1)
        dropped = (row[:, q * lanes : (q + 1) * lanes] < 0.5) & (count < DROP - 0.5)
        key = jnp.where(dropped, -1.0, tile - jnp.minimum(count, float(DROP)))
        picks.append(jnp.where(slot == key, 1.0, 0.0).astype(BF16))
    fetch_amp.wait()
    tiles = [amp_in[:, q * lanes * TW : (q + 1) * lanes * TW].astype(F32).reshape(lanes, TW).astype(BF16) for q in range(4)]
    packs = [dot(picks[q], tiles[q]).astype(BF16) for q in range(4)]
    for q in range(4):
        for i in range(16):
            for k in range(CAP // 4):
                at = i * CT + k * 4
                packed_out[q * 16 + i, :, k * TW : (k + 1) * TW] = packs[q][at : at + 4, :]
    store = pltpu.make_async_copy(packed_out, out_ref, out_sem)
    store.start()
    store.wait()


def pack(live, amplitudes):
    lanes = 2 * TW
    anywhere = pl.BlockSpec(memory_space=pl.ANY)
    return pl.pallas_call(
        pack_kernel,
        out_shape=jax.ShapeDtypeStruct((NW, 4, CAP // 4 * TW), BF16),
        in_specs=[anywhere, anywhere],
        out_specs=anywhere,
        scratch_shapes=[
            pltpu.VMEM((8, NW * CT), jnp.int32),
            pltpu.VMEM((1, NW * CT * TW), BF16),
            pltpu.VMEM((NW, 4, CAP // 4 * TW), BF16),
            pltpu.SemaphoreType.DMA,
            pltpu.SemaphoreType.DMA,
            pltpu.SemaphoreType.DMA,
        ],
        name="pack",
    )(live, amplitudes)


def whole(*dims):
    return pl.BlockSpec(dims, lambda i, *ids: (0,) * len(dims))


def codes_kernel(ids_ref, live_ref, out_ref):
    wide, core = ids_ref[0], ids_ref[1]
    rows = NX * NW
    r, g = iota((rows, 512), 0), iota((rows, 512), 1)
    rx, ry, rz = r >> 6, (r >> 4) & 3, r & 15
    source = (rz << 5) + (ry << 3) + (rx << 1) + core
    pick = jnp.where(g == source, 1.0, 0.0).astype(BF16)
    live = dot(pick, live_ref[...].astype(F32).astype(BF16)).astype(BF16)
    base = (wide % 8) * CT
    lane, c = iota((TW, TW), 0), iota((TW, TW), 1)
    take = jnp.where((lane == base + c) & (c < CT), 1.0, 0.0).astype(BF16)
    prior = jnp.where((lane >= base) & (lane < base + c) & (c < CT), 1.0, 0.0).astype(BF16)
    here = dot(live, take)
    count = dot((1.0 - live.astype(F32)).astype(BF16), prior)
    code = jnp.where(here > 0.5, jnp.minimum(count, float(DROP)), 9.0).astype(BF16)
    spread_row, spread_col = iota((TW, CT * TW), 0), iota((TW, CT * TW), 1)
    spread = jnp.where(spread_row == spread_col // TW, 1.0, 0.0).astype(BF16)
    out_ref[...] = dot(code, spread).astype(BF16)


def codes_of(ids, live):
    return pl.pallas_call(
        codes_kernel,
        out_shape=jax.ShapeDtypeStruct((NX * NW, CT * TW), BF16),
        grid_spec=pltpu.PrefetchScalarGridSpec(
            num_scalar_prefetch=1,
            grid=(1,),
            in_specs=[pl.BlockSpec((512, TW), lambda i, ids: (0, ids[0] // 8))],
            out_specs=whole(NX * NW, CT * TW),
        ),
        name="codes",
    )(ids, live)


def ladder_kernel(code_ref, amp_ref, own_ref, other_ref, out_ref):
    core = lax.axis_index("c")
    rows = NX * NW
    slots = [
        jnp.concatenate([amp_ref[x * 4 + j % 4, :, j // 4 * TW : (j // 4 + 1) * TW] for x in range(NX)])
        for j in range(CAP)
    ]
    sums = [None, None]
    for first in range(0, CT, 2):
        values = []
        for t in (first, first + 1):
            code_t = code_ref[:, t * TW : (t + 1) * TW]
            value = jnp.zeros((rows, TW), BF16)
            for d in range(DROP + 1):
                if 0 <= t - d < CAP:
                    value = jnp.where(code_t == d, slots[t - d], value)
            values.append(value)
        used = jnp.concatenate(values, axis=1)
        for i, ref in enumerate((own_ref, other_ref)):
            part = ref[:, first * TW : (first + 2) * TW]
            more = lax.dot_general(used, part, (((1,), (1,)), ((), ())), preferred_element_type=F32)
            sums[i] = more if sums[i] is None else sums[i] + more
    for total, column in ((sums[0], core), (sums[1], 1 - core)):
        for i in range(NX * NY):
            for h in range(2):
                out_ref[i, column * 2 + h] = total[i * NZ : (i + 1) * NZ, h * TW : (h + 1) * TW]


def ladder(codes, amp, own, other):
    return pl.pallas_call(
        ladder_kernel,
        out_shape=jax.ShapeDtypeStruct((NY * NX, 2 * NC, NZ, TW), F32),
        compiler_params=pltpu.CompilerParams(vmem_limit_bytes=40 * 1024 * 1024),
        name="ladder",
    )(codes, amp, own, other)


def per_device(amplitudes, amplitude_live, integrals, integral_live):
    mask = integral_live.astype(BF16)
    own = (integrals.reshape(2, TW, CT, TW) * mask[:, None, :, None]).reshape(2 * TW, CT * TW)
    other = lax.ppermute(own, "c", [(0, 1), (1, 0)])
    packed = pack(amplitude_live, amplitudes)
    arrived = lax.all_to_all(packed, ("z", "y"), 0, 0, tiled=True)
    slots = arrived.reshape(NZ, NY, 4, CAP // 4 * TW).transpose(2, 1, 0, 3).reshape(4, NW, CAP // 4 * TW)
    gathered = lax.all_gather(slots, "x", axis=0, tiled=True)
    ids = jnp.stack([own_wide(), lax.axis_index("c")])
    sums = ladder(codes_of(ids, amplitude_live), gathered, own, other)
    sums = lax.all_to_all(sums, ("x", "y"), 0, 0, tiled=True)
    sums = sums.reshape(NX, NY, 2 * NC, NZ, TW).sum(axis=1)
    sums = sums.reshape(16, NZ, TW).transpose(1, 0, 2)
    sums = lax.all_to_all(sums, "z", 0, 0, tiled=True).sum(axis=0)
    sums = lax.optimization_barrier(sums.reshape(1, NX * NC * 256))
    return sums.astype(BF16)


def solution(mesh):
    fine = Mesh(mesh.devices.reshape(NZ, NY, NX, NC), ("z", "y", "x", "c"))
    wide, grp = ("z", "y"), ("x", "c")
    return jax.shard_map(
        per_device,
        mesh=fine,
        in_specs=(P(wide + grp, None), P(), P(grp, wide), P(grp, wide)),
        out_specs=P(wide + grp, None),
        check_vma=False,
    )
```

```python
import functools

import jax
import jax.numpy as jnp
from jax import lax
from jax.experimental import pallas as pl
from jax.experimental.pallas import tpu as pltpu
from jax.sharding import Mesh, PartitionSpec as P

TW = 128
NZ, NY, NX, NC = 16, 4, 4, 2
NW = NZ * NY
CT = 16
CAP = 12
DROP = CT - CAP
F32 = jnp.float32
BF16 = jnp.bfloat16


def iota(shape, dim):
    return lax.broadcasted_iota(jnp.int32, shape, dim)


def dot(a, b):
    return lax.dot_general(a, b, (((1,), (0,)), ((), ())), preferred_element_type=F32)


def before_matrix():
    rows, cols = iota((TW, TW), 0), iota((TW, TW), 1)
    same = (rows >> 4) == (cols >> 4)
    return jnp.where(same & (rows < cols), 1.0, 0.0).astype(BF16)


def own_wide():
    return lax.axis_index("z") * NY + lax.axis_index("y")


def pack_kernel(live_ref, amp_ref, out_ref, live_in, amp_in, packed_out, live_sem, amp_sem, out_sem):
    lanes = 2 * TW
    block = pl.multiple_of(own_wide() * 8, 8)
    fetch_live = pltpu.make_async_copy(live_ref.at[pl.ds(block, 8)], live_in, live_sem)
    fetch_live.start()
    fetch_amp = pltpu.make_async_copy(amp_ref, amp_in, amp_sem)
    fetch_amp.start()
    before = before_matrix()
    out_row, col = iota((lanes, lanes), 0), iota((lanes, lanes), 1)
    slot = jnp.where(out_row >> 4 == col >> 4, out_row & 15, -7).astype(F32)
    tile = (iota((1, lanes), 1) & 15).astype(F32)
    fetch_live.wait()
    live = live_in[...].astype(F32)
    sub = lax.axis_index("x") * NC + lax.axis_index("c")
    row = jnp.sum(jnp.where(iota(live.shape, 0) == sub, live, 0.0), axis=0, keepdims=True)
    dead = jnp.broadcast_to(1.0 - row, (8, NW * CT)).astype(BF16)
    blocks = jnp.concatenate([dead[:, j * TW : (j + 1) * TW] for j in range(8)], axis=0)
    counts = dot(blocks, before)
    picks = []
    for q in range(4):
        count = jnp.concatenate([counts[16 * q : 16 * q + 1], counts[16 * q + 8 : 16 * q + 9]], axis=1)
        dropped = (row[:, q * lanes : (q + 1) * lanes] < 0.5) & (count < DROP - 0.5)
        key = jnp.where(dropped, -1.0, tile - jnp.minimum(count, float(DROP)))
        picks.append(jnp.where(slot == key, 1.0, 0.0).astype(BF16))
    fetch_amp.wait()
    tiles = [amp_in[:, q * lanes * TW : (q + 1) * lanes * TW].astype(F32).reshape(lanes, TW).astype(BF16) for q in range(4)]
    packs = [dot(picks[q], tiles[q]).astype(BF16) for q in range(4)]
    for q in range(4):
        for i in range(16):
            for k in range(CAP // 4):
                at = i * CT + k * 4
                packed_out[q * 16 + i, :, k * TW : (k + 1) * TW] = packs[q][at : at + 4, :]
    store = pltpu.make_async_copy(packed_out, out_ref, out_sem)
    store.start()
    store.wait()


def pack(live, amplitudes):
    lanes = 2 * TW
    anywhere = pl.BlockSpec(memory_space=pl.ANY)
    return pl.pallas_call(
        pack_kernel,
        out_shape=jax.ShapeDtypeStruct((NW, 4, CAP // 4 * TW), BF16),
        in_specs=[anywhere, anywhere],
        out_specs=anywhere,
        scratch_shapes=[
            pltpu.VMEM((8, NW * CT), jnp.int32),
            pltpu.VMEM((1, NW * CT * TW), BF16),
            pltpu.VMEM((NW, 4, CAP // 4 * TW), BF16),
            pltpu.SemaphoreType.DMA,
            pltpu.SemaphoreType.DMA,
            pltpu.SemaphoreType.DMA,
        ],
        name="pack",
    )(live, amplitudes)


def whole(*dims):
    return pl.BlockSpec(dims, lambda i, *ids: (0,) * len(dims))


def codes_kernel(ids_ref, live_ref, out_ref):
    wide, core = ids_ref[0], ids_ref[1]
    rows = NX * NW
    r, g = iota((rows, 512), 0), iota((rows, 512), 1)
    rx, ry, rz = r >> 6, (r >> 4) & 3, r & 15
    source = (rz << 5) + (ry << 3) + (rx << 1) + core
    pick = jnp.where(g == source, 1.0, 0.0).astype(BF16)
    live = dot(pick, live_ref[...].astype(F32).astype(BF16)).astype(BF16)
    base = (wide % 8) * CT
    lane, c = iota((TW, TW), 0), iota((TW, TW), 1)
    take = jnp.where((lane == base + c) & (c < CT), 1.0, 0.0).astype(BF16)
    prior = jnp.where((lane >= base) & (lane < base + c) & (c < CT), 1.0, 0.0).astype(BF16)
    here = dot(live, take)
    count = dot((1.0 - live.astype(F32)).astype(BF16), prior)
    code = jnp.where(here > 0.5, jnp.minimum(count, float(DROP)), 9.0).astype(BF16)
    spread_row, spread_col = iota((TW, CT * TW), 0), iota((TW, CT * TW), 1)
    spread = jnp.where(spread_row == spread_col // TW, 1.0, 0.0).astype(BF16)
    out_ref[...] = dot(code, spread).astype(BF16)


def codes_of(ids, live):
    return pl.pallas_call(
        codes_kernel,
        out_shape=jax.ShapeDtypeStruct((NX * NW, CT * TW), BF16),
        grid_spec=pltpu.PrefetchScalarGridSpec(
            num_scalar_prefetch=1,
            grid=(1,),
            in_specs=[pl.BlockSpec((512, TW), lambda i, ids: (0, ids[0] // 8))],
            out_specs=whole(NX * NW, CT * TW),
        ),
        name="codes",
    )(ids, live)


def ladder_kernel(code_ref, amp_ref, own_ref, other_ref, out_ref):
    core = lax.axis_index("c")
    rows = NX * NW
    slots = [
        jnp.concatenate([amp_ref[x * 4 + j % 4, :, j // 4 * TW : (j // 4 + 1) * TW] for x in range(NX)])
        for j in range(CAP)
    ]
    sums = [None, None]
    for first in range(0, CT, 4):
        values = []
        for t in range(first, first + 4):
            code_t = code_ref[:, t * TW : (t + 1) * TW]
            value = jnp.zeros((rows, TW), BF16)
            for d in range(DROP + 1):
                if 0 <= t - d < CAP:
                    value = jnp.where(code_t == d, slots[t - d], value)
            values.append(value)
        used = jnp.concatenate(values, axis=1)
        for i, ref in enumerate((own_ref, other_ref)):
            part = ref[:, first * TW : (first + 4) * TW]
            more = lax.dot_general(used, part, (((1,), (1,)), ((), ())), preferred_element_type=F32)
            sums[i] = more if sums[i] is None else sums[i] + more
    for total, column in ((sums[0], core), (sums[1], 1 - core)):
        for i in range(NX * NY):
            for h in range(2):
                out_ref[i, column * 2 + h] = total[i * NZ : (i + 1) * NZ, h * TW : (h + 1) * TW]


def ladder(codes, amp, own, other):
    return pl.pallas_call(
        ladder_kernel,
        out_shape=jax.ShapeDtypeStruct((NY * NX, 2 * NC, NZ, TW), F32),
        compiler_params=pltpu.CompilerParams(vmem_limit_bytes=40 * 1024 * 1024),
        name="ladder",
    )(codes, amp, own, other)


def per_device(amplitudes, amplitude_live, integrals, integral_live):
    mask = integral_live.astype(BF16)
    own = (integrals.reshape(2, TW, CT, TW) * mask[:, None, :, None]).reshape(2 * TW, CT * TW)
    other = lax.ppermute(own, "c", [(0, 1), (1, 0)])
    packed = pack(amplitude_live, amplitudes)
    arrived = lax.all_to_all(packed, ("z", "y"), 0, 0, tiled=True)
    slots = arrived.reshape(NZ, NY, 4, CAP // 4 * TW).transpose(2, 1, 0, 3).reshape(4, NW, CAP // 4 * TW)
    gathered = lax.all_gather(slots, "x", axis=0, tiled=True)
    ids = jnp.stack([own_wide(), lax.axis_index("c")])
    sums = ladder(codes_of(ids, amplitude_live), gathered, own, other)
    sums = lax.all_to_all(sums, ("x", "y"), 0, 0, tiled=True)
    sums = sums.reshape(NX, NY, 2 * NC, NZ, TW).sum(axis=1)
    sums = sums.reshape(16, NZ, TW).transpose(1, 0, 2)
    sums = lax.all_to_all(sums, "z", 0, 0, tiled=True).sum(axis=0)
    sums = lax.optimization_barrier(sums.reshape(1, NX * NC * 256))
    return sums.astype(BF16)


def solution(mesh):
    fine = Mesh(mesh.devices.reshape(NZ, NY, NX, NC), ("z", "y", "x", "c"))
    wide, grp = ("z", "y"), ("x", "c")
    return jax.shard_map(
        per_device,
        mesh=fine,
        in_specs=(P(wide + grp, None), P(), P(grp, wide), P(grp, wide)),
        out_specs=P(wide + grp, None),
        check_vma=False,
    )
```
